32 devices in a mesh: dp: 2 (over x), expert: 16 (over z, y, core).
Axes of the slice: x: 2, y: 2, z: 4, core: 2. Of those that a mesh axis runs over, the one named last changes fastest.
Arguments:
- tokens: bfloat16 [4096, 1024], P(('dp', 'expert')), may hold values from -6 to 6
- cotangent: bfloat16 [4096, 1024], P(('dp', 'expert')), may hold values from -6 to 6
- expert_ids: int32 [4096, 6], P(('dp', 'expert')), may hold values from 0 to 15, all different within a row; in each aligned block of 128 rows (0 to 127, 128 to 255, ...) at most 60 rows name the same one
- gate_weights: float32 [4096, 6], P(('dp', 'expert')), may hold values from 0.05 to 0.3
- partner: int32 [16], replicated, may hold values from 0 to 15, as said below
- weights: bfloat16 [16, 1024, 3, 384], P('expert', 'dp'), may hold values from -0.3125 to 0.3125
- first_moment: bfloat16 [16, 1024, 3, 384], P('expert', 'dp'), may hold values from -6 to 6
- second_moment: bfloat16 [16, 1024, 3, 384], P('expert', 'dp'), may hold values from 0.099609375 to 4
Outputs:
- mixed: bfloat16 [4096, 1024], P(('dp', 'expert'))
- token_grad: bfloat16 [4096, 1024], P(('dp', 'expert'))
- new_weights: bfloat16 [16, 1024, 3, 384], P('expert', 'dp')
- new_first: bfloat16 [16, 1024, 3, 384], P('expert', 'dp')
- new_second: bfloat16 [16, 1024, 3, 384], P('expert', 'dp')
The draws below stay inside these ranges and needn't reach their ends.
Inputs may be any that keep to these rules, and one draw needn't show every extreme that they name: `expert_ids`: each row names 6 different experts. Among the 128 tokens of one device (aligned blocks of rows), no expert is named by more than 60 tokens, and in every draw some block names some expert exactly 60 times. partner[partner[h]] = h and partner[h] != h for every h.
All inputs are finite; a program needn't handle non-finite values.
Results may differ from the reference program's by a relative error of at most 0.024.
Values may be sent and summed in bfloat16 or wider, within the bound.
A program may use at most 64 MiB of HBM per device.

```python
import math
import jax
import jax.numpy as jnp
import numpy as np
from jax import lax

D = 1024
FF = 384
TOP = 6
TOK_DEV = 128
EXPERTS = 16
CAP = 60
TOKENS = 4096
N_DP = 2
N_EXPERT = 16


def draw_partner(key, part):
    order = jax.random.permutation(key, EXPERTS).astype(jnp.int32)
    paired = order.reshape(EXPERTS // 2, 2)[:, ::-1].reshape(EXPERTS)
    return jnp.zeros((EXPERTS,), jnp.int32).at[order].set(paired)


def levels(own_key, dims, pieces, least, top_value):
    def one(axis_at, shards_of):
        heights = jax.random.uniform(jax.random.fold_in(jax.random.fold_in(own_key, 6), axis_at), (shards_of,), jnp.float32, least / len(pieces), top_value / len(pieces))
        return jnp.repeat(jnp.exp(heights), dims[axis_at] // shards_of).reshape((-1,) + (1,) * (len(dims) - axis_at - 1))

    factor_of = one(*pieces[0])
    for cut in pieces[1:]:
        factor_of = factor_of * one(*cut)
    return factor_of


def routed_block(own_key, own, number, rows, count, top, bound, lean):
    order = jax.random.permutation(own_key, count)
    packed, usual = load_shares(count, rows * top, bound, lean, True), load_shares(count, rows * top, bound, lean, False)
    places = jnp.arange(count)

    def named(lengths, turn):
        used = int((lengths > 0).sum())
        fixed = max(1, used // 4)
        shifted = fixed + (places - fixed + turn * (used - fixed)) % max(1, count - fixed)
        return jnp.zeros((count,), jnp.int32).at[order[jnp.where(places < fixed, places, shifted)]].set(jnp.asarray(lengths, jnp.int32))

    lengths = jnp.where(number % 4 == 0, named(packed, number // 4), named(usual, number - number // 4 - 1))
    mixed = jax.random.permutation(jax.random.fold_in(own, 3), count)
    giver, taker = mixed[0:count // 2 * 2:2], mixed[1:count // 2 * 2:2]
    slack = jnp.minimum(lengths[giver] - 1, bound - lengths[taker]) // 2
    slack = jnp.where((giver == order[0]) | (taker == order[0]) | (lengths[taker] == 0), 0, jnp.maximum(slack, 0))
    shifted = jax.random.randint(jax.random.fold_in(own, 4), (count // 2,), 0, 1 << 20) % (slack + 1)
    lengths = lengths.at[giver].add(-shifted).at[taker].add(shifted)
    members = jnp.searchsorted(jnp.cumsum(lengths), jnp.arange(rows * top), side="right").astype(jnp.int32)
    listing = members.reshape(top, rows).T
    listing = listing[jax.random.permutation(jax.random.fold_in(own, 1), rows)]
    turn = jax.random.randint(jax.random.fold_in(own, 2), (rows, 1), 0, top)
    return jnp.take_along_axis(listing, (jnp.arange(top)[None, :] + turn) % top, axis=1)


def load_shares(count, total, reach, skew, full):
    weights = [(1 << 20) // math.isqrt(standing ** skew) + 1 for standing in range(1, count + 1)]
    largest = reach if full else min(reach, max(-(-total // count), total * weights[0] // sum(weights)))
    least = 1 if total - largest >= count - 1 else 0
    holding, rest = [largest] + [least] * (count - 1), total - largest - least * (count - 1)
    while rest > 0:
        free = [i for i in range(1, count) if holding[i] < largest] or [i for i in range(1, count) if holding[i] < reach]
        mass, remaining = sum([weights[i] for i in free]), rest
        for i in free:
            addition = min(reach - holding[i], max(1, remaining * weights[i] // mass), rest)
            holding[i] = holding[i] + addition
            rest = rest - addition
    return np.array(holding)


def normal_values(stream_key, shape, scale, bound, shards=(), kind=jnp.bfloat16):
    factor_of = levels(stream_key, shape, shards, -0.22, 0.18) if shards else 1.0
    array = jax.random.normal(stream_key, shape, jnp.float32) * scale * factor_of
    return jnp.minimum(jnp.maximum(array, -bound), bound).astype(kind)


def setup_inputs(seed: int = 0) -> dict:
    seeds = jax.random.split(jax.random.key(seed), 9)
    tokens = normal_values(seeds[0], (TOKENS, D), 1.0, 6.0, ((0, 32),))
    cotangent = normal_values(seeds[1], (TOKENS, D), 1.0, 6.0, ((0, 32),))
    expert_ids_keys = jax.random.split(jax.random.fold_in(seeds[2], 1), TOKENS // TOK_DEV)
    expert_ids_turns = jax.random.permutation(jax.random.fold_in(seeds[2], 3), TOKENS // TOK_DEV)
    expert_ids = jax.vmap(lambda own, number: routed_block(jax.random.fold_in(seeds[2], 2), own, number, TOK_DEV, EXPERTS, TOP, CAP, 1))(expert_ids_keys, expert_ids_turns).reshape((TOKENS, TOP))
    gate_weights = jnp.clip(0.05 + 0.25 * jax.random.uniform(seeds[3], (TOKENS, TOP), jnp.float32) ** levels(seeds[3], (TOKENS, TOP), ((0, 32),), -0.2, 0.2), 0.05, 0.3)
    partner = draw_partner(jax.random.fold_in(seeds[8], 71), 0)
    weights = normal_values(seeds[5], (EXPERTS, D, 3, FF), FF ** -0.5, 0.3125, ((0, 16), (1, 2)))
    first_moment = normal_values(seeds[6], (EXPERTS, D, 3, FF), 1.0, 6.0, ((0, 16), (1, 2)))
    second_moment = jnp.clip(jnp.exp(math.log(4.0) - 3.6927934 * jax.random.uniform(seeds[7], (EXPERTS, D, 3, FF), jnp.float32) ** levels(seeds[7], (EXPERTS, D, 3, FF), ((0, 16), (1, 2)), -0.2, 0.2)), 0.099609375, 4.0).astype(jnp.bfloat16)
    return {"tokens": tokens, "cotangent": cotangent, "expert_ids": expert_ids, "gate_weights": gate_weights, "partner": partner, "weights": weights, "first_moment": first_moment, "second_moment": second_moment}


beta_one = 0.9
beta_two = 0.95
learn_rate = 0.01
decay_rate = 0.1
eps_adam = 1e-08
step_count = 100

def expert_pass(x_rows, dy_rows, expert_w):
    hidden_width = expert_w.shape[2]
    gate_up = expert_w[:, 0:2, :].reshape(expert_w.shape[0], 2 * hidden_width)
    down_proj = expert_w[:, 2, :]
    both_proj = jnp.dot(x_rows, gate_up, preferred_element_type=jnp.float32)
    pre_act = both_proj[:, :hidden_width]
    lin_act = both_proj[:, hidden_width:]
    sigmoid_pre = jax.nn.sigmoid(pre_act)
    silu_pre = pre_act * sigmoid_pre
    hidden = (silu_pre * lin_act).astype(jnp.bfloat16)
    out_rows = jnp.dot(hidden, down_proj.T, preferred_element_type=jnp.float32).astype(jnp.bfloat16)
    hidden_grad = jnp.dot(dy_rows, down_proj, preferred_element_type=jnp.float32)
    pre_grad = (hidden_grad * lin_act * sigmoid_pre * (1.0 + pre_act * (1.0 - sigmoid_pre))).astype(jnp.bfloat16)
    lin_grad = (hidden_grad * silu_pre).astype(jnp.bfloat16)
    both_grad = jnp.concatenate([pre_grad, lin_grad], axis=1)
    item_grad = jnp.dot(both_grad, gate_up.T, preferred_element_type=jnp.float32).astype(jnp.bfloat16)
    proj_grad = jnp.dot(x_rows.T, both_grad, preferred_element_type=jnp.float32)
    down_grad = jnp.dot(dy_rows.T, hidden, preferred_element_type=jnp.float32)
    partial_grad = jnp.concatenate([proj_grad.reshape(-1, 2, hidden_width), down_grad.reshape(-1, 1, hidden_width)], axis=1)
    return (out_rows, item_grad, partial_grad)

def reference(tokens, cotangent, expert_ids, gate_weights, partner, weights, first_moment, second_moment):
    model_width = tokens.shape[1]
    hidden_width = weights.shape[3]
    per_replica = N_EXPERT * TOK_DEV
    item_total = per_replica * TOP
    slot_total = N_EXPERT * CAP
    zero_row = jnp.zeros((1, model_width), jnp.bfloat16)
    accum_rows = N_DP * (per_replica + 1)

    def one_expert(carry, expert):
        mixed_acc, grad_acc = carry
        expert_w = lax.dynamic_index_in_dim(weights, expert, 0, keepdims=False)
        grad_sum = jnp.zeros((model_width, 3, hidden_width), jnp.float32)
        for replica in range(N_DP):
            low = replica * per_replica
            flat_ids = expert_ids[low:low + per_replica].reshape(item_total)
            chosen = jnp.nonzero(flat_ids == expert, size=slot_total, fill_value=item_total)[0].astype(jnp.int32)
            token_of = (chosen // TOP).astype(jnp.int32)
            x_pad = jnp.concatenate([tokens[low:low + per_replica], zero_row], axis=0)
            cot_pad = jnp.concatenate([cotangent[low:low + per_replica], zero_row], axis=0)
            gate_pad = jnp.concatenate([gate_weights[low:low + per_replica].reshape(item_total), jnp.zeros((1,), jnp.float32)])
            gate_rows = gate_pad[chosen]
            x_rows = x_pad[token_of]
            dy_rows = (gate_rows[:, None] * cot_pad[token_of].astype(jnp.float32)).astype(jnp.bfloat16)
            out_rows, item_grad, partial_grad = expert_pass(x_rows, dy_rows, expert_w)
            target = token_of + replica * (per_replica + 1)
            out_back = lax.optimization_barrier(out_rows).astype(jnp.float32)
            grad_back = lax.optimization_barrier(item_grad).astype(jnp.float32)
            mixed_acc = mixed_acc.at[target].add(gate_rows[:, None] * out_back)
            grad_acc = grad_acc.at[target].add(grad_back)
            rounded = lax.optimization_barrier(partial_grad.astype(jnp.bfloat16))
            grad_sum = grad_sum + rounded.astype(jnp.float32)
        w_old = expert_w.astype(jnp.float32)
        m_old = lax.dynamic_index_in_dim(first_moment, expert, 0, keepdims=False).astype(jnp.float32)
        v_old = lax.dynamic_index_in_dim(second_moment, expert, 0, keepdims=False).astype(jnp.float32)
        m_new = beta_one * m_old + (1.0 - beta_one) * grad_sum
        v_new = beta_two * v_old + (1.0 - beta_two) * grad_sum * grad_sum
        m_hat = m_new / (1.0 - beta_one ** step_count)
        v_hat = v_new / (1.0 - beta_two ** step_count)
        w_new = w_old - learn_rate * (m_hat / (jnp.sqrt(v_hat) + eps_adam) + decay_rate * w_old)
        states = (w_new.astype(jnp.bfloat16), m_new.astype(jnp.bfloat16), v_new.astype(jnp.bfloat16))
        return ((mixed_acc, grad_acc), states)
    start = (jnp.zeros((accum_rows, model_width), jnp.float32), jnp.zeros((accum_rows, model_width), jnp.float32))
    (mixed_acc, grad_acc), states = lax.scan(one_expert, start, jnp.arange(EXPERTS, dtype=jnp.int32))
    mixed = mixed_acc.reshape(N_DP, per_replica + 1, model_width)[:, :per_replica].reshape(TOKENS, model_width)
    token_grad = grad_acc.reshape(N_DP, per_replica + 1, model_width)[:, :per_replica].reshape(TOKENS, model_width)
    new_weights = states[0][partner]
    new_first = states[1][partner]
    new_second = states[2][partner]
    return (mixed.astype(jnp.bfloat16), token_grad.astype(jnp.bfloat16), new_weights, new_first, new_second)
```

```python
import jax
import jax.numpy as jnp
from jax import lax
from jax.sharding import PartitionSpec as P

beta_one = 0.9
beta_two = 0.95
learn_rate = 0.01
decay_rate = 0.1
eps_adam = 1e-08
step_count = 100


def send_rows(parts):
    return (lax.all_to_all(parts[0], "expert", split_axis=0, concat_axis=0, tiled=True),)


def send_back(parts):
    return (lax.all_to_all(parts[0], "expert", split_axis=0, concat_axis=0, tiled=True),)


def shards_by_slot(
    tokens, cotangent, expert_ids, gate_weights, partner, weights, first_moment, second_moment
):
    experts_here = lax.axis_size("expert")
    tok_dev, model_width = tokens.shape
    top_count = expert_ids.shape[1]
    hidden_width = weights.shape[3]
    capacity = min(tok_dev, max(2, 5 * tok_dev * top_count // (4 * experts_here)))
    item_total = tok_dev * top_count
    slot_total = experts_here * capacity
    flat_ids = expert_ids.reshape(item_total)
    onehot = (flat_ids[:, None] == jnp.arange(experts_here, dtype=jnp.int32)[None, :]).astype(
        jnp.int32
    )
    before = jnp.cumsum(onehot, axis=0) - onehot
    slot_of = jnp.sum(before * onehot, axis=1)
    position = flat_ids * capacity + slot_of
    source = (
        jnp.full((slot_total,), item_total, jnp.int32)
        .at[position]
        .set(jnp.arange(item_total, dtype=jnp.int32))
    )
    token_of = source // top_count
    zero_row = jnp.zeros((1, model_width), jnp.bfloat16)
    x_send = jnp.concatenate([tokens, zero_row], axis=0)[token_of].reshape(
        experts_here, capacity, model_width
    )
    gate_flat = gate_weights.reshape(item_total)
    gate_pad = jnp.concatenate([gate_flat, jnp.zeros((1,), jnp.float32)])
    cot_rows = jnp.concatenate([cotangent, zero_row], axis=0)[token_of].astype(jnp.float32)
    dy_send = (
        (gate_pad[source][:, None] * cot_rows)
        .astype(jnp.bfloat16)
        .reshape(experts_here, capacity, model_width)
    )
    gathered = lax.all_gather(weights, "dp", axis=1, tiled=True)[0]
    gate_up = gathered[:, 0:2, :].reshape(model_width, 2 * hidden_width)
    down_proj = gathered[:, 2, :]
    block_shape = (experts_here, capacity, model_width)
    (x_recv,) = send_rows((x_send,))
    forward_x_rows = x_recv.reshape(slot_total, model_width)
    both_proj = jnp.dot(forward_x_rows, gate_up, preferred_element_type=jnp.float32)
    pre_act = both_proj[:, :hidden_width]
    lin_act = both_proj[:, hidden_width:]
    sigmoid_pre = jax.nn.sigmoid(pre_act)
    silu_pre = pre_act * sigmoid_pre
    forward_hidden = (silu_pre * lin_act).astype(jnp.bfloat16)
    out_rows = jnp.dot(forward_hidden, down_proj.T, preferred_element_type=jnp.float32).astype(
        jnp.bfloat16
    )
    x_rows, saved, hidden, out_rows = (
        forward_x_rows,
        (pre_act, lin_act, sigmoid_pre, silu_pre),
        forward_hidden,
        out_rows,
    )
    (out_back,) = send_back((out_rows.reshape(block_shape),))
    (dy_recv,) = send_rows((dy_send,))
    pre_act, lin_act, sigmoid_pre, silu_pre = saved
    backward_dy_rows = dy_recv.reshape(slot_total, model_width)
    hidden_grad = jnp.dot(backward_dy_rows, down_proj, preferred_element_type=jnp.float32)
    pre_grad = (hidden_grad * lin_act * sigmoid_pre * (1.0 + pre_act * (1.0 - sigmoid_pre))).astype(
        jnp.bfloat16
    )
    lin_grad = (hidden_grad * silu_pre).astype(jnp.bfloat16)
    backward_both_grad = jnp.concatenate([pre_grad, lin_grad], axis=1)
    item_grad = jnp.dot(backward_both_grad, gate_up.T, preferred_element_type=jnp.float32).astype(
        jnp.bfloat16
    )
    dy_rows, both_grad, item_grad = (backward_dy_rows, backward_both_grad, item_grad)
    (grad_back,) = send_back((item_grad.reshape(block_shape),))
    out_items = (
        out_back.reshape(slot_total, model_width)[position].astype(jnp.float32) * gate_flat[:, None]
    )
    mixed = jnp.sum(out_items.reshape(tok_dev, top_count, model_width), axis=1).astype(jnp.bfloat16)
    grad_items = grad_back.reshape(slot_total, model_width)[position].astype(jnp.float32)
    token_grad = jnp.sum(grad_items.reshape(tok_dev, top_count, model_width), axis=1).astype(
        jnp.bfloat16
    )
    count = lax.axis_size("dp") * weights.shape[1]
    proj_grad = jnp.dot(x_rows.T, both_grad, preferred_element_type=jnp.float32)
    down_grad = jnp.dot(dy_rows.T, hidden, preferred_element_type=jnp.float32)
    grad_sum = lax.psum_scatter(
        jnp.concatenate(
            [proj_grad.reshape(count, 2, hidden_width), down_grad.reshape(count, 1, hidden_width)],
            axis=1,
        ).astype(jnp.bfloat16),
        "dp",
        scatter_dimension=0,
        tiled=True,
    ).astype(jnp.float32)
    w_old = weights[0].astype(jnp.float32)
    m_old = first_moment[0].astype(jnp.float32)
    v_old = second_moment[0].astype(jnp.float32)
    m_new = beta_one * m_old + (1.0 - beta_one) * grad_sum
    v_new = beta_two * v_old + (1.0 - beta_two) * grad_sum * grad_sum
    m_hat = m_new / (1.0 - beta_one**step_count)
    v_hat = v_new / (1.0 - beta_two**step_count)
    w_new = w_old - learn_rate * (m_hat / (jnp.sqrt(v_hat) + eps_adam) + decay_rate * w_old)
    pieces = (
        w_new.astype(jnp.bfloat16).reshape(experts_here, -1),
        m_new.astype(jnp.bfloat16).reshape(experts_here, -1),
        v_new.astype(jnp.bfloat16).reshape(experts_here, -1),
    )
    spread = (
        lax.all_to_all(pieces[0], "expert", split_axis=0, concat_axis=0, tiled=True),
        lax.all_to_all(pieces[1], "expert", split_axis=0, concat_axis=0, tiled=True),
        lax.all_to_all(pieces[2], "expert", split_axis=0, concat_axis=0, tiled=True),
    )
    ordered = (spread[0][partner], spread[1][partner], spread[2][partner])
    homed = (
        lax.all_to_all(ordered[0], "expert", split_axis=0, concat_axis=0, tiled=True),
        lax.all_to_all(ordered[1], "expert", split_axis=0, concat_axis=0, tiled=True),
        lax.all_to_all(ordered[2], "expert", split_axis=0, concat_axis=0, tiled=True),
    )
    new_weights = homed[0].reshape(weights.shape)
    new_first = homed[1].reshape(weights.shape)
    new_second = homed[2].reshape(weights.shape)
    return (mixed, token_grad, new_weights, new_first, new_second)


def adam(w_old, m_old, v_old, grad_sum):
    m_new = beta_one * m_old + (1.0 - beta_one) * grad_sum
    v_new = beta_two * v_old + (1.0 - beta_two) * grad_sum * grad_sum
    m_hat = m_new / (1.0 - beta_one**step_count)
    v_hat = v_new / (1.0 - beta_two**step_count)
    w_new = w_old - learn_rate * (m_hat / (jnp.sqrt(v_hat) + eps_adam) + decay_rate * w_old)
    return w_new, m_new, v_new


def shards_dense(
    tokens, cotangent, expert_ids, gate_weights, partner, weights, first_moment, second_moment
):
    experts_here = lax.axis_size("expert")
    me = lax.axis_index("expert")
    tok_dev, model_width = tokens.shape
    own_rows, hidden_width = weights.shape[1], weights.shape[3]
    width = 3 * hidden_width
    f32, bf16 = jnp.float32, jnp.bfloat16
    hits = expert_ids[:, :, None] == jnp.arange(experts_here, dtype=jnp.int32)[None, None, :]
    gate_table = jnp.sum(jnp.where(hits, gate_weights[:, :, None], 0.0), axis=1).T
    w_flat = weights[0].reshape(own_rows, width)
    gathered = lax.all_gather(w_flat, "dp", axis=0, tiled=True)
    x_rows = lax.all_gather(tokens, "expert", axis=0, tiled=True)
    cot_rows = lax.all_gather(cotangent, "expert", axis=0, tiled=True)
    gate_all = lax.all_gather(gate_table, "expert", axis=0)
    gate = lax.dynamic_index_in_dim(gate_all, me, 1, keepdims=False)
    gate = gate.reshape(experts_here * tok_dev, 1)
    gate_up = gathered[:, : 2 * hidden_width]
    down_proj = gathered[:, 2 * hidden_width :]
    both_proj = jnp.dot(x_rows, gate_up, preferred_element_type=f32)
    pre_act = both_proj[:, :hidden_width]
    lin_act = both_proj[:, hidden_width:]
    sigmoid_pre = jax.nn.sigmoid(pre_act)
    silu_pre = pre_act * sigmoid_pre
    hidden = (silu_pre * lin_act).astype(bf16)
    out_rows = jnp.dot(hidden, down_proj.T, preferred_element_type=f32)
    mixed = lax.psum_scatter(
        (gate * out_rows).astype(bf16), "expert", scatter_dimension=0, tiled=True
    )
    dy_rows = (gate * cot_rows.astype(f32)).astype(bf16)
    hidden_grad = jnp.dot(dy_rows, down_proj, preferred_element_type=f32)
    pre_grad = hidden_grad * lin_act * sigmoid_pre * (1.0 + pre_act * (1.0 - sigmoid_pre))
    lin_grad = hidden_grad * silu_pre
    both_grad = jnp.concatenate([pre_grad.astype(bf16), lin_grad.astype(bf16)], axis=1)
    proj_grad = jnp.dot(x_rows.T, both_grad, preferred_element_type=f32)
    down_grad = jnp.dot(dy_rows.T, hidden, preferred_element_type=f32)
    partial = jnp.concatenate([proj_grad.astype(bf16), down_grad.astype(bf16)], axis=1)
    grad_sum = lax.psum_scatter(partial, "dp", scatter_dimension=0, tiled=True).astype(f32)
    item_grad = jnp.dot(both_grad, gate_up.T, preferred_element_type=f32).astype(bf16)
    token_grad = lax.psum_scatter(item_grad, "expert", scatter_dimension=0, tiled=True)
    m_flat = first_moment[0].reshape(own_rows, width)
    v_flat = second_moment[0].reshape(own_rows, width)
    new_state = adam(w_flat.astype(f32), m_flat.astype(f32), v_flat.astype(f32), grad_sum)
    share = own_rows // experts_here
    outs = []
    for part in new_state:
        pieces = part.astype(bf16).reshape(experts_here, share, width)
        spread = lax.all_to_all(pieces, "expert", split_axis=0, concat_axis=0, tiled=True)
        homed = lax.all_to_all(
            spread[partner], "expert", split_axis=0, concat_axis=0, tiled=True
        )
        outs.append(homed.reshape(weights.shape))
    return (mixed, token_grad, *outs)


def shards(*args):
    replica_rows = lax.axis_size("expert") * args[0].shape[0]
    if replica_rows <= 4096 and args[5].shape[1] % (16 * lax.axis_size("expert")) == 0:
        return shards_dense(*args)
    return shards_by_slot(*args)


def solution(mesh):
    in_specs = (
        P(("dp", "expert"), None),
        P(("dp", "expert"), None),
        P(("dp", "expert"), None),
        P(("dp", "expert"), None),
        P(),
        P("expert", "dp", None, None),
        P("expert", "dp", None, None),
        P("expert", "dp", None, None),
    )
    out_specs = (
        P(("dp", "expert"), None),
        P(("dp", "expert"), None),
        P("expert", "dp", None, None),
        P("expert", "dp", None, None),
        P("expert", "dp", None, None),
    )
    return jax.shard_map(shards, mesh=mesh, in_specs=in_specs, out_specs=out_specs, check_vma=False)
```

```python
import functools

import jax
import jax.numpy as jnp
from jax import lax
from jax.experimental import pallas as pl
from jax.experimental.pallas import tpu as pltpu
from jax.sharding import PartitionSpec as P

beta_one = 0.9
beta_two = 0.95
learn_rate = 0.01
decay_rate = 0.1
eps_adam = 1e-08
step_count = 100


def send_rows(parts):
    return (lax.all_to_all(parts[0], "expert", split_axis=0, concat_axis=0, tiled=True),)


def send_back(parts):
    return (lax.all_to_all(parts[0], "expert", split_axis=0, concat_axis=0, tiled=True),)


def shards_by_slot(
    tokens, cotangent, expert_ids, gate_weights, partner, weights, first_moment, second_moment
):
    experts_here = lax.axis_size("expert")
    tok_dev, model_width = tokens.shape
    top_count = expert_ids.shape[1]
    hidden_width = weights.shape[3]
    capacity = min(tok_dev, max(2, 5 * tok_dev * top_count // (4 * experts_here)))
    item_total = tok_dev * top_count
    slot_total = experts_here * capacity
    flat_ids = expert_ids.reshape(item_total)
    onehot = (flat_ids[:, None] == jnp.arange(experts_here, dtype=jnp.int32)[None, :]).astype(
        jnp.int32
    )
    before = jnp.cumsum(onehot, axis=0) - onehot
    slot_of = jnp.sum(before * onehot, axis=1)
    position = flat_ids * capacity + slot_of
    source = (
        jnp.full((slot_total,), item_total, jnp.int32)
        .at[position]
        .set(jnp.arange(item_total, dtype=jnp.int32))
    )
    token_of = source // top_count
    zero_row = jnp.zeros((1, model_width), jnp.bfloat16)
    x_send = jnp.concatenate([tokens, zero_row], axis=0)[token_of].reshape(
        experts_here, capacity, model_width
    )
    gate_flat = gate_weights.reshape(item_total)
    gate_pad = jnp.concatenate([gate_flat, jnp.zeros((1,), jnp.float32)])
    cot_rows = jnp.concatenate([cotangent, zero_row], axis=0)[token_of].astype(jnp.float32)
    dy_send = (
        (gate_pad[source][:, None] * cot_rows)
        .astype(jnp.bfloat16)
        .reshape(experts_here, capacity, model_width)
    )
    gathered = lax.all_gather(weights, "dp", axis=1, tiled=True)[0]
    gate_up = gathered[:, 0:2, :].reshape(model_width, 2 * hidden_width)
    down_proj = gathered[:, 2, :]
    block_shape = (experts_here, capacity, model_width)
    (x_recv,) = send_rows((x_send,))
    forward_x_rows = x_recv.reshape(slot_total, model_width)
    both_proj = jnp.dot(forward_x_rows, gate_up, preferred_element_type=jnp.float32)
    pre_act = both_proj[:, :hidden_width]
    lin_act = both_proj[:, hidden_width:]
    sigmoid_pre = jax.nn.sigmoid(pre_act)
    silu_pre = pre_act * sigmoid_pre
    forward_hidden = (silu_pre * lin_act).astype(jnp.bfloat16)
    out_rows = jnp.dot(forward_hidden, down_proj.T, preferred_element_type=jnp.float32).astype(
        jnp.bfloat16
    )
    x_rows, saved, hidden, out_rows = (
        forward_x_rows,
        (pre_act, lin_act, sigmoid_pre, silu_pre),
        forward_hidden,
        out_rows,
    )
    (out_back,) = send_back((out_rows.reshape(block_shape),))
    (dy_recv,) = send_rows((dy_send,))
    pre_act, lin_act, sigmoid_pre, silu_pre = saved
    backward_dy_rows = dy_recv.reshape(slot_total, model_width)
    hidden_grad = jnp.dot(backward_dy_rows, down_proj, preferred_element_type=jnp.float32)
    pre_grad = (hidden_grad * lin_act * sigmoid_pre * (1.0 + pre_act * (1.0 - sigmoid_pre))).astype(
        jnp.bfloat16
    )
    lin_grad = (hidden_grad * silu_pre).astype(jnp.bfloat16)
    backward_both_grad = jnp.concatenate([pre_grad, lin_grad], axis=1)
    item_grad = jnp.dot(backward_both_grad, gate_up.T, preferred_element_type=jnp.float32).astype(
        jnp.bfloat16
    )
    dy_rows, both_grad, item_grad = (backward_dy_rows, backward_both_grad, item_grad)
    (grad_back,) = send_back((item_grad.reshape(block_shape),))
    out_items = (
        out_back.reshape(slot_total, model_width)[position].astype(jnp.float32) * gate_flat[:, None]
    )
    mixed = jnp.sum(out_items.reshape(tok_dev, top_count, model_width), axis=1).astype(jnp.bfloat16)
    grad_items = grad_back.reshape(slot_total, model_width)[position].astype(jnp.float32)
    token_grad = jnp.sum(grad_items.reshape(tok_dev, top_count, model_width), axis=1).astype(
        jnp.bfloat16
    )
    count = lax.axis_size("dp") * weights.shape[1]
    proj_grad = jnp.dot(x_rows.T, both_grad, preferred_element_type=jnp.float32)
    down_grad = jnp.dot(dy_rows.T, hidden, preferred_element_type=jnp.float32)
    grad_sum = lax.psum_scatter(
        jnp.concatenate(
            [proj_grad.reshape(count, 2, hidden_width), down_grad.reshape(count, 1, hidden_width)],
            axis=1,
        ).astype(jnp.bfloat16),
        "dp",
        scatter_dimension=0,
        tiled=True,
    ).astype(jnp.float32)
    w_old = weights[0].astype(jnp.float32)
    m_old = first_moment[0].astype(jnp.float32)
    v_old = second_moment[0].astype(jnp.float32)
    m_new = beta_one * m_old + (1.0 - beta_one) * grad_sum
    v_new = beta_two * v_old + (1.0 - beta_two) * grad_sum * grad_sum
    m_hat = m_new / (1.0 - beta_one**step_count)
    v_hat = v_new / (1.0 - beta_two**step_count)
    w_new = w_old - learn_rate * (m_hat / (jnp.sqrt(v_hat) + eps_adam) + decay_rate * w_old)
    pieces = (
        w_new.astype(jnp.bfloat16).reshape(experts_here, -1),
        m_new.astype(jnp.bfloat16).reshape(experts_here, -1),
        v_new.astype(jnp.bfloat16).reshape(experts_here, -1),
    )
    spread = (
        lax.all_to_all(pieces[0], "expert", split_axis=0, concat_axis=0, tiled=True),
        lax.all_to_all(pieces[1], "expert", split_axis=0, concat_axis=0, tiled=True),
        lax.all_to_all(pieces[2], "expert", split_axis=0, concat_axis=0, tiled=True),
    )
    ordered = (spread[0][partner], spread[1][partner], spread[2][partner])
    homed = (
        lax.all_to_all(ordered[0], "expert", split_axis=0, concat_axis=0, tiled=True),
        lax.all_to_all(ordered[1], "expert", split_axis=0, concat_axis=0, tiled=True),
        lax.all_to_all(ordered[2], "expert", split_axis=0, concat_axis=0, tiled=True),
    )
    new_weights = homed[0].reshape(weights.shape)
    new_first = homed[1].reshape(weights.shape)
    new_second = homed[2].reshape(weights.shape)
    return (mixed, token_grad, new_weights, new_first, new_second)


def adam(w_old, m_old, v_old, grad_sum):
    m_new = beta_one * m_old + (1.0 - beta_one) * grad_sum
    v_new = beta_two * v_old + (1.0 - beta_two) * grad_sum * grad_sum
    m_hat = m_new / (1.0 - beta_one**step_count)
    v_hat = v_new / (1.0 - beta_two**step_count)
    w_new = w_old - learn_rate * (m_hat / (jnp.sqrt(v_hat) + eps_adam) + decay_rate * w_old)
    return w_new, m_new, v_new


def move_kernel(n, count, with_table, *refs):
    partner_ref, refs = refs[0], refs[1:]
    states, refs = refs[:count], refs[count:]
    if with_table:
        table_ref, refs = refs[0], refs[1:]
    homes, refs = refs[:count], refs[count:]
    if with_table:
        table_out, refs = refs[0], refs[1:]
    spread, refs = refs[:count], refs[count:]
    ordered, send_one, recv_one, send_two, recv_two = refs[:5]
    me = lax.axis_index("expert")
    share = states[0].shape[1] // n

    def rows(number):
        return pl.ds(pl.multiple_of(number * share, share), share)

    def to_peer(src, dst, send_sem, recv_sem, step):
        return pltpu.make_async_remote_copy(
            src_ref=src,
            dst_ref=dst,
            send_sem=send_sem,
            recv_sem=recv_sem,
            device_id={"expert": lax.rem(me + step, n)},
            device_id_type=pl.DeviceIdType.MESH,
        )

    def table_copy(step):
        peer = lax.rem(me + step, n)
        return to_peer(
            table_ref.at[peer], table_out.at[me], refs[5].at[step], refs[6].at[step], step
        )

    def first(i, step):
        peer = lax.rem(me + step, n)
        return to_peer(
            states[i].at[:, rows(peer), :],
            spread[i].at[me],
            send_one.at[i, step],
            recv_one.at[i, step],
            step,
        )

    def second(i, step):
        peer = lax.rem(me + step, n)
        return to_peer(
            ordered.at[i, peer],
            homes[i].at[:, rows(me), :],
            send_two.at[i, step],
            recv_two.at[i, step],
            step,
        )

    def each(fn):
        def body(step, carry):
            fn(step)
            return carry

        lax.fori_loop(1, n, body, 0)

    barrier = pltpu.get_barrier_semaphore()
    each(
        lambda step: pl.semaphore_signal(
            barrier,
            inc=1,
            device_id={"expert": lax.rem(me + step, n)},
            device_id_type=pl.DeviceIdType.MESH,
        )
    )
    pl.semaphore_wait(barrier, n - 1)
    if with_table:
        each(lambda step: table_copy(step).start())
        table_out[me] = table_ref[me]
    for i in range(count):
        each(lambda step: first(i, step).start())
    for i in range(count):
        spread[i][me] = states[i][:, rows(me), :]
        each(lambda step: first(i, step).wait_recv())

        def pick(home, carry):
            ordered[i, home] = spread[i][partner_ref[home]]
            return carry

        lax.fori_loop(0, n, pick, 0)
        each(lambda step: second(i, step).start())
        homes[i][:, rows(me), :] = ordered[i, me]
    if with_table:
        each(lambda step: table_copy(step).wait())
    for i in range(count):
        each(lambda step: first(i, step).wait_send())
        each(lambda step: second(i, step).wait())


def move_states(states, partner, table, number):
    n = lax.axis_size("expert")
    count = len(states)
    planes, own_rows, width = states[0].shape
    share = own_rows // n
    vmem = pl.BlockSpec(memory_space=pltpu.VMEM)
    extra = [] if table is None else [table]
    sems = [pltpu.SemaphoreType.DMA((count, n))] * 4
    sems += [pltpu.SemaphoreType.DMA((n,))] * (2 * len(extra))
    moved = 2 * count * planes * own_rows * width * 2
    return pl.pallas_call(
        functools.partial(move_kernel, n, count, bool(extra)),
        out_shape=[jax.ShapeDtypeStruct(a.shape, a.dtype) for a in [*states, *extra]],
        in_specs=[pl.BlockSpec(memory_space=pltpu.SMEM)] + [vmem] * (count + len(extra)),
        out_specs=[vmem] * (count + len(extra)),
        scratch_shapes=[
            *[pltpu.VMEM((n, planes, share, width), jnp.bfloat16)] * count,
            pltpu.VMEM((count, n, planes, share, width), jnp.bfloat16),
            *sems,
        ],
        compiler_params=pltpu.CompilerParams(
            collective_id=number, has_side_effects=True, vmem_limit_bytes=32 * 2**20
        ),
        cost_estimate=pl.CostEstimate(
            flops=0, bytes_accessed=30 * moved, transcendentals=0
        ),
    )(partner, *states, *extra)


def shards_dense(
    tokens, cotangent, expert_ids, gate_weights, partner, weights, first_moment, second_moment
):
    experts_here = lax.axis_size("expert")
    tok_dev, model_width = tokens.shape
    own_rows, hidden_width = weights.shape[1], weights.shape[3]
    f32, bf16 = jnp.float32, jnp.bfloat16
    hits = expert_ids[:, :, None] == jnp.arange(experts_here, dtype=jnp.int32)[None, None, :]
    gate_table = jnp.sum(jnp.where(hits, gate_weights[:, :, None], 0.0), axis=1).T
    gate_table = jnp.broadcast_to(gate_table[:, None, :], (experts_here, 8, tok_dev))
    old = [a[0].transpose(1, 0, 2) for a in (weights, first_moment, second_moment)]
    gathered = lax.all_gather(old[0], "dp", axis=1, tiled=True)
    x_rows = lax.all_gather(tokens, "expert", axis=0, tiled=True)
    cot_rows = lax.all_gather(cotangent, "expert", axis=0, tiled=True)
    *old_here, gate_all = move_states(old, partner, gate_table, 0)
    gate = gate_all[:, 0, :].reshape(experts_here * tok_dev, 1)
    gate_up = jnp.concatenate([gathered[0], gathered[1]], axis=1)
    down_proj = gathered[2]
    both_proj = jnp.dot(x_rows, gate_up, preferred_element_type=f32)
    pre_act = both_proj[:, :hidden_width]
    lin_act = both_proj[:, hidden_width:]
    sigmoid_pre = jax.nn.sigmoid(pre_act)
    silu_pre = pre_act * sigmoid_pre
    hidden = (silu_pre * lin_act).astype(bf16)
    dy_rows = (gate * cot_rows.astype(f32)).astype(bf16)
    hidden_grad = jnp.dot(dy_rows, down_proj, preferred_element_type=f32)
    pre_grad = hidden_grad * lin_act * sigmoid_pre * (1.0 + pre_act * (1.0 - sigmoid_pre))
    pre_grad = pre_grad.astype(bf16)
    lin_grad = (hidden_grad * silu_pre).astype(bf16)
    both_grad = jnp.concatenate([pre_grad, lin_grad], axis=1)
    proj_grad = jnp.dot(x_rows.T, both_grad, preferred_element_type=f32).astype(bf16)
    down_grad = jnp.dot(dy_rows.T, hidden, preferred_element_type=f32).astype(bf16)
    partial = jnp.stack([proj_grad[:, :hidden_width], proj_grad[:, hidden_width:], down_grad])
    grad_sum = lax.psum_scatter(partial, "dp", scatter_dimension=1, tiled=True)
    out_rows = jnp.dot(hidden, down_proj.T, preferred_element_type=f32)
    mixed = lax.psum_scatter(
        (gate * out_rows).astype(bf16), "expert", scatter_dimension=0, tiled=True
    )
    item_grad = jnp.dot(both_grad, gate_up.T, preferred_element_type=f32).astype(bf16)
    token_grad = lax.psum_scatter(item_grad, "expert", scatter_dimension=0, tiled=True)
    (grad_here,) = move_states([grad_sum], partner, None, 1)
    new_state = adam(*[a.astype(f32) for a in old_here], grad_here.astype(f32))
    outs = [a.astype(bf16).transpose(1, 0, 2)[None] for a in new_state]
    return (mixed, token_grad, *outs)


def shards(*args):
    replica_rows = lax.axis_size("expert") * args[0].shape[0]
    if replica_rows <= 4096 and args[5].shape[1] % (16 * lax.axis_size("expert")) == 0:
        return shards_dense(*args)
    return shards_by_slot(*args)


def solution(mesh):
    in_specs = (
        P(("dp", "expert"), None),
        P(("dp", "expert"), None),
        P(("dp", "expert"), None),
        P(("dp", "expert"), None),
        P(),
        P("expert", "dp", None, None),
        P("expert", "dp", None, None),
        P("expert", "dp", None, None),
    )
    out_specs = (
        P(("dp", "expert"), None),
        P(("dp", "expert"), None),
        P("expert", "dp", None, None),
        P("expert", "dp", None, None),
        P("expert", "dp", None, None),
    )
    return jax.shard_map(shards, mesh=mesh, in_specs=in_specs, out_specs=out_specs, check_vma=False)
```

```python
import functools

import jax
import jax.numpy as jnp
from jax import lax
from jax.experimental import pallas as pl
from jax.experimental.pallas import tpu as pltpu
from jax.sharding import PartitionSpec as P

beta_one = 0.9
beta_two = 0.95
learn_rate = 0.01
decay_rate = 0.1
eps_adam = 1e-08
step_count = 100


def send_rows(parts):
    return (lax.all_to_all(parts[0], "expert", split_axis=0, concat_axis=0, tiled=True),)


def send_back(parts):
    return (lax.all_to_all(parts[0], "expert", split_axis=0, concat_axis=0, tiled=True),)


def shards_by_slot(
    tokens, cotangent, expert_ids, gate_weights, partner, weights, first_moment, second_moment
):
    experts_here = lax.axis_size("expert")
    tok_dev, model_width = tokens.shape
    top_count = expert_ids.shape[1]
    hidden_width = weights.shape[3]
    capacity = min(tok_dev, max(2, 5 * tok_dev * top_count // (4 * experts_here)))
    item_total = tok_dev * top_count
    slot_total = experts_here * capacity
    flat_ids = expert_ids.reshape(item_total)
    onehot = (flat_ids[:, None] == jnp.arange(experts_here, dtype=jnp.int32)[None, :]).astype(
        jnp.int32
    )
    before = jnp.cumsum(onehot, axis=0) - onehot
    slot_of = jnp.sum(before * onehot, axis=1)
    position = flat_ids * capacity + slot_of
    source = (
        jnp.full((slot_total,), item_total, jnp.int32)
        .at[position]
        .set(jnp.arange(item_total, dtype=jnp.int32))
    )
    token_of = source // top_count
    zero_row = jnp.zeros((1, model_width), jnp.bfloat16)
    x_send = jnp.concatenate([tokens, zero_row], axis=0)[token_of].reshape(
        experts_here, capacity, model_width
    )
    gate_flat = gate_weights.reshape(item_total)
    gate_pad = jnp.concatenate([gate_flat, jnp.zeros((1,), jnp.float32)])
    cot_rows = jnp.concatenate([cotangent, zero_row], axis=0)[token_of].astype(jnp.float32)
    dy_send = (
        (gate_pad[source][:, None] * cot_rows)
        .astype(jnp.bfloat16)
        .reshape(experts_here, capacity, model_width)
    )
    gathered = lax.all_gather(weights, "dp", axis=1, tiled=True)[0]
    gate_up = gathered[:, 0:2, :].reshape(model_width, 2 * hidden_width)
    down_proj = gathered[:, 2, :]
    block_shape = (experts_here, capacity, model_width)
    (x_recv,) = send_rows((x_send,))
    forward_x_rows = x_recv.reshape(slot_total, model_width)
    both_proj = jnp.dot(forward_x_rows, gate_up, preferred_element_type=jnp.float32)
    pre_act = both_proj[:, :hidden_width]
    lin_act = both_proj[:, hidden_width:]
    sigmoid_pre = jax.nn.sigmoid(pre_act)
    silu_pre = pre_act * sigmoid_pre
    forward_hidden = (silu_pre * lin_act).astype(jnp.bfloat16)
    out_rows = jnp.dot(forward_hidden, down_proj.T, preferred_element_type=jnp.float32).astype(
        jnp.bfloat16
    )
    x_rows, saved, hidden, out_rows = (
        forward_x_rows,
        (pre_act, lin_act, sigmoid_pre, silu_pre),
        forward_hidden,
        out_rows,
    )
    (out_back,) = send_back((out_rows.reshape(block_shape),))
    (dy_recv,) = send_rows((dy_send,))
    pre_act, lin_act, sigmoid_pre, silu_pre = saved
    backward_dy_rows = dy_recv.reshape(slot_total, model_width)
    hidden_grad = jnp.dot(backward_dy_rows, down_proj, preferred_element_type=jnp.float32)
    pre_grad = (hidden_grad * lin_act * sigmoid_pre * (1.0 + pre_act * (1.0 - sigmoid_pre))).astype(
        jnp.bfloat16
    )
    lin_grad = (hidden_grad * silu_pre).astype(jnp.bfloat16)
    backward_both_grad = jnp.concatenate([pre_grad, lin_grad], axis=1)
    item_grad = jnp.dot(backward_both_grad, gate_up.T, preferred_element_type=jnp.float32).astype(
        jnp.bfloat16
    )
    dy_rows, both_grad, item_grad = (backward_dy_rows, backward_both_grad, item_grad)
    (grad_back,) = send_back((item_grad.reshape(block_shape),))
    out_items = (
        out_back.reshape(slot_total, model_width)[position].astype(jnp.float32) * gate_flat[:, None]
    )
    mixed = jnp.sum(out_items.reshape(tok_dev, top_count, model_width), axis=1).astype(jnp.bfloat16)
    grad_items = grad_back.reshape(slot_total, model_width)[position].astype(jnp.float32)
    token_grad = jnp.sum(grad_items.reshape(tok_dev, top_count, model_width), axis=1).astype(
        jnp.bfloat16
    )
    count = lax.axis_size("dp") * weights.shape[1]
    proj_grad = jnp.dot(x_rows.T, both_grad, preferred_element_type=jnp.float32)
    down_grad = jnp.dot(dy_rows.T, hidden, preferred_element_type=jnp.float32)
    grad_sum = lax.psum_scatter(
        jnp.concatenate(
            [proj_grad.reshape(count, 2, hidden_width), down_grad.reshape(count, 1, hidden_width)],
            axis=1,
        ).astype(jnp.bfloat16),
        "dp",
        scatter_dimension=0,
        tiled=True,
    ).astype(jnp.float32)
    w_old = weights[0].astype(jnp.float32)
    m_old = first_moment[0].astype(jnp.float32)
    v_old = second_moment[0].astype(jnp.float32)
    m_new = beta_one * m_old + (1.0 - beta_one) * grad_sum
    v_new = beta_two * v_old + (1.0 - beta_two) * grad_sum * grad_sum
    m_hat = m_new / (1.0 - beta_one**step_count)
    v_hat = v_new / (1.0 - beta_two**step_count)
    w_new = w_old - learn_rate * (m_hat / (jnp.sqrt(v_hat) + eps_adam) + decay_rate * w_old)
    pieces = (
        w_new.astype(jnp.bfloat16).reshape(experts_here, -1),
        m_new.astype(jnp.bfloat16).reshape(experts_here, -1),
        v_new.astype(jnp.bfloat16).reshape(experts_here, -1),
    )
    spread = (
        lax.all_to_all(pieces[0], "expert", split_axis=0, concat_axis=0, tiled=True),
        lax.all_to_all(pieces[1], "expert", split_axis=0, concat_axis=0, tiled=True),
        lax.all_to_all(pieces[2], "expert", split_axis=0, concat_axis=0, tiled=True),
    )
    ordered = (spread[0][partner], spread[1][partner], spread[2][partner])
    homed = (
        lax.all_to_all(ordered[0], "expert", split_axis=0, concat_axis=0, tiled=True),
        lax.all_to_all(ordered[1], "expert", split_axis=0, concat_axis=0, tiled=True),
        lax.all_to_all(ordered[2], "expert", split_axis=0, concat_axis=0, tiled=True),
    )
    new_weights = homed[0].reshape(weights.shape)
    new_first = homed[1].reshape(weights.shape)
    new_second = homed[2].reshape(weights.shape)
    return (mixed, token_grad, new_weights, new_first, new_second)


def adam(w_old, m_old, v_old, grad_sum):
    m_new = beta_one * m_old + (1.0 - beta_one) * grad_sum
    v_new = beta_two * v_old + (1.0 - beta_two) * grad_sum * grad_sum
    m_hat = m_new / (1.0 - beta_one**step_count)
    v_hat = v_new / (1.0 - beta_two**step_count)
    w_new = w_old - learn_rate * (m_hat / (jnp.sqrt(v_hat) + eps_adam) + decay_rate * w_old)
    return w_new, m_new, v_new


def move_kernel(n, count, with_table, *refs):
    partner_ref, refs = refs[0], refs[1:]
    states, refs = refs[:count], refs[count:]
    if with_table:
        table_ref, refs = refs[0], refs[1:]
    homes, refs = refs[:count], refs[count:]
    if with_table:
        table_out, refs = refs[0], refs[1:]
    spread, refs = refs[:count], refs[count:]
    ordered, send_one, recv_one, send_two, recv_two = refs[:5]
    me = lax.axis_index("expert")
    share = states[0].shape[1] // n

    def rows(number):
        return pl.ds(pl.multiple_of(number * share, share), share)

    def to_peer(src, dst, send_sem, recv_sem, step):
        return pltpu.make_async_remote_copy(
            src_ref=src,
            dst_ref=dst,
            send_sem=send_sem,
            recv_sem=recv_sem,
            device_id={"expert": lax.rem(me + step, n)},
            device_id_type=pl.DeviceIdType.MESH,
        )

    def table_copy(step):
        peer = lax.rem(me + step, n)
        return to_peer(
            table_ref.at[peer], table_out.at[me], refs[5].at[step], refs[6].at[step], step
        )

    def first(i, step):
        peer = lax.rem(me + step, n)
        return to_peer(
            states[i].at[:, rows(peer), :],
            spread[i].at[me],
            send_one.at[i, step],
            recv_one.at[i, step],
            step,
        )

    def second(i, step):
        peer = lax.rem(me + step, n)
        return to_peer(
            ordered.at[i, peer],
            homes[i].at[:, rows(me), :],
            send_two.at[i, step],
            recv_two.at[i, step],
            step,
        )

    def each(fn):
        def body(step, carry):
            fn(step)
            return carry

        lax.fori_loop(1, n, body, 0)

    barrier = pltpu.get_barrier_semaphore()
    each(
        lambda step: pl.semaphore_signal(
            barrier,
            inc=1,
            device_id={"expert": lax.rem(me + step, n)},
            device_id_type=pl.DeviceIdType.MESH,
        )
    )
    pl.semaphore_wait(barrier, n - 1)
    if with_table:
        each(lambda step: table_copy(step).start())
        table_out[me] = table_ref[me]
    for i in range(count):
        each(lambda step: first(i, step).start())
    for i in range(count):
        spread[i][me] = states[i][:, rows(me), :]
        each(lambda step: first(i, step).wait_recv())

        def pick(home, carry):
            ordered[i, home] = spread[i][partner_ref[home]]
            return carry

        lax.fori_loop(0, n, pick, 0)
        each(lambda step: second(i, step).start())
        homes[i][:, rows(me), :] = ordered[i, me]
    if with_table:
        each(lambda step: table_copy(step).wait())
    for i in range(count):
        each(lambda step: first(i, step).wait_send())
        each(lambda step: second(i, step).wait())


def move_states(states, partner, table, number):
    n = lax.axis_size("expert")
    count = len(states)
    planes, own_rows, width = states[0].shape
    share = own_rows // n
    vmem = pl.BlockSpec(memory_space=pltpu.VMEM)
    extra = [] if table is None else [table]
    sems = [pltpu.SemaphoreType.DMA((count, n))] * 4
    sems += [pltpu.SemaphoreType.DMA((n,))] * (2 * len(extra))
    moved = 2 * count * planes * own_rows * width * 2
    return pl.pallas_call(
        functools.partial(move_kernel, n, count, bool(extra)),
        out_shape=[jax.ShapeDtypeStruct(a.shape, a.dtype) for a in [*states, *extra]],
        in_specs=[pl.BlockSpec(memory_space=pltpu.SMEM)] + [vmem] * (count + len(extra)),
        out_specs=[vmem] * (count + len(extra)),
        scratch_shapes=[
            *[pltpu.VMEM((n, planes, share, width), jnp.bfloat16)] * count,
            pltpu.VMEM((count, n, planes, share, width), jnp.bfloat16),
            *sems,
        ],
        compiler_params=pltpu.CompilerParams(
            collective_id=number, has_side_effects=True, vmem_limit_bytes=32 * 2**20
        ),
        cost_estimate=pl.CostEstimate(
            flops=0, bytes_accessed=30 * moved, transcendentals=0
        ),
    )(partner, *states, *extra)


def shards_dense(
    tokens, cotangent, expert_ids, gate_weights, partner, weights, first_moment, second_moment
):
    experts_here = lax.axis_size("expert")
    tok_dev, model_width = tokens.shape
    own_rows, hidden_width = weights.shape[1], weights.shape[3]
    f32, bf16 = jnp.float32, jnp.bfloat16
    hits = expert_ids[:, :, None] == jnp.arange(experts_here, dtype=jnp.int32)[None, None, :]
    gate_table = jnp.sum(jnp.where(hits, gate_weights[:, :, None], 0.0), axis=1).T
    gate_table = jnp.broadcast_to(gate_table[:, None, :], (experts_here, 8, tok_dev))
    old = [a[0].transpose(1, 0, 2) for a in (weights, first_moment, second_moment)]
    gathered = lax.all_gather(old[0], "dp", axis=1, tiled=True)
    x_rows = lax.all_gather(tokens, "expert", axis=0, tiled=True)
    cot_rows = lax.all_gather(cotangent, "expert", axis=0, tiled=True)
    w_here, m_here, gate_all = move_states(old[:2], partner, gate_table, 0)
    gate = gate_all[:, 0, :].reshape(experts_here * tok_dev, 1)
    gate_up = jnp.concatenate([gathered[0], gathered[1]], axis=1)
    down_proj = gathered[2]
    both_proj = jnp.dot(x_rows, gate_up, preferred_element_type=f32)
    pre_act = both_proj[:, :hidden_width]
    lin_act = both_proj[:, hidden_width:]
    sigmoid_pre = jax.nn.sigmoid(pre_act)
    silu_pre = pre_act * sigmoid_pre
    hidden = (silu_pre * lin_act).astype(bf16)
    out_rows = jnp.dot(hidden, down_proj.T, preferred_element_type=f32)
    out_part = (gate * out_rows).astype(bf16)
    out_part, v_old = lax.optimization_barrier((out_part, old[2]))
    mixed = lax.psum_scatter(out_part, "expert", scatter_dimension=0, tiled=True)
    (v_here,) = move_states([v_old], partner, None, 2)
    gate, v_here = lax.optimization_barrier((gate, v_here))
    dy_rows = (gate * cot_rows.astype(f32)).astype(bf16)
    hidden_grad = jnp.dot(dy_rows, down_proj, preferred_element_type=f32)
    pre_grad = hidden_grad * lin_act * sigmoid_pre * (1.0 + pre_act * (1.0 - sigmoid_pre))
    pre_grad = pre_grad.astype(bf16)
    lin_grad = (hidden_grad * silu_pre).astype(bf16)
    both_grad = jnp.concatenate([pre_grad, lin_grad], axis=1)
    proj_grad = jnp.dot(x_rows.T, both_grad, preferred_element_type=f32).astype(bf16)
    down_grad = jnp.dot(dy_rows.T, hidden, preferred_element_type=f32).astype(bf16)
    partial = jnp.stack([proj_grad[:, :hidden_width], proj_grad[:, hidden_width:], down_grad])
    partial, mixed = lax.optimization_barrier((partial, mixed))
    grad_sum = lax.psum_scatter(partial, "dp", scatter_dimension=1, tiled=True)
    item_grad = jnp.dot(both_grad, gate_up.T, preferred_element_type=f32).astype(bf16)
    token_grad = lax.psum_scatter(item_grad, "expert", scatter_dimension=0, tiled=True)
    (grad_here,) = move_states([grad_sum], partner, None, 1)
    new_state = adam(*[a.astype(f32) for a in (w_here, m_here, v_here)], grad_here.astype(f32))
    outs = [a.astype(bf16).transpose(1, 0, 2)[None] for a in new_state]
    return (mixed, token_grad, *outs)


def shards(*args):
    replica_rows = lax.axis_size("expert") * args[0].shape[0]
    if replica_rows <= 4096 and args[5].shape[1] % (16 * lax.axis_size("expert")) == 0:
        return shards_dense(*args)
    return shards_by_slot(*args)


def solution(mesh):
    in_specs = (
        P(("dp", "expert"), None),
        P(("dp", "expert"), None),
        P(("dp", "expert"), None),
        P(("dp", "expert"), None),
        P(),
        P("expert", "dp", None, None),
        P("expert", "dp", None, None),
        P("expert", "dp", None, None),
    )
    out_specs = (
        P(("dp", "expert"), None),
        P(("dp", "expert"), None),
        P("expert", "dp", None, None),
        P("expert", "dp", None, None),
        P("expert", "dp", None, None),
    )
    return jax.shard_map(shards, mesh=mesh, in_specs=in_specs, out_specs=out_specs, check_vma=False)
```

```python
import functools

import jax
import jax.numpy as jnp
from jax import lax
from jax.experimental import pallas as pl
from jax.experimental.pallas import tpu as pltpu
from jax.sharding import PartitionSpec as P

beta_one = 0.9
beta_two = 0.95
learn_rate = 0.01
decay_rate = 0.1
eps_adam = 1e-08
step_count = 100


def send_rows(parts):
    return (lax.all_to_all(parts[0], "expert", split_axis=0, concat_axis=0, tiled=True),)


def send_back(parts):
    return (lax.all_to_all(parts[0], "expert", split_axis=0, concat_axis=0, tiled=True),)


def shards_by_slot(
    tokens, cotangent, expert_ids, gate_weights, partner, weights, first_moment, second_moment
):
    experts_here = lax.axis_size("expert")
    tok_dev, model_width = tokens.shape
    top_count = expert_ids.shape[1]
    hidden_width = weights.shape[3]
    capacity = min(tok_dev, max(2, 5 * tok_dev * top_count // (4 * experts_here)))
    item_total = tok_dev * top_count
    slot_total = experts_here * capacity
    flat_ids = expert_ids.reshape(item_total)
    onehot = (flat_ids[:, None] == jnp.arange(experts_here, dtype=jnp.int32)[None, :]).astype(
        jnp.int32
    )
    before = jnp.cumsum(onehot, axis=0) - onehot
    slot_of = jnp.sum(before * onehot, axis=1)
    position = flat_ids * capacity + slot_of
    source = (
        jnp.full((slot_total,), item_total, jnp.int32)
        .at[position]
        .set(jnp.arange(item_total, dtype=jnp.int32))
    )
    token_of = source // top_count
    zero_row = jnp.zeros((1, model_width), jnp.bfloat16)
    x_send = jnp.concatenate([tokens, zero_row], axis=0)[token_of].reshape(
        experts_here, capacity, model_width
    )
    gate_flat = gate_weights.reshape(item_total)
    gate_pad = jnp.concatenate([gate_flat, jnp.zeros((1,), jnp.float32)])
    cot_rows = jnp.concatenate([cotangent, zero_row], axis=0)[token_of].astype(jnp.float32)
    dy_send = (
        (gate_pad[source][:, None] * cot_rows)
        .astype(jnp.bfloat16)
        .reshape(experts_here, capacity, model_width)
    )
    gathered = lax.all_gather(weights, "dp", axis=1, tiled=True)[0]
    gate_up = gathered[:, 0:2, :].reshape(model_width, 2 * hidden_width)
    down_proj = gathered[:, 2, :]
    block_shape = (experts_here, capacity, model_width)
    (x_recv,) = send_rows((x_send,))
    forward_x_rows = x_recv.reshape(slot_total, model_width)
    both_proj = jnp.dot(forward_x_rows, gate_up, preferred_element_type=jnp.float32)
    pre_act = both_proj[:, :hidden_width]
    lin_act = both_proj[:, hidden_width:]
    sigmoid_pre = jax.nn.sigmoid(pre_act)
    silu_pre = pre_act * sigmoid_pre
    forward_hidden = (silu_pre * lin_act).astype(jnp.bfloat16)
    out_rows = jnp.dot(forward_hidden, down_proj.T, preferred_element_type=jnp.float32).astype(
        jnp.bfloat16
    )
    x_rows, saved, hidden, out_rows = (
        forward_x_rows,
        (pre_act, lin_act, sigmoid_pre, silu_pre),
        forward_hidden,
        out_rows,
    )
    (out_back,) = send_back((out_rows.reshape(block_shape),))
    (dy_recv,) = send_rows((dy_send,))
    pre_act, lin_act, sigmoid_pre, silu_pre = saved
    backward_dy_rows = dy_recv.reshape(slot_total, model_width)
    hidden_grad = jnp.dot(backward_dy_rows, down_proj, preferred_element_type=jnp.float32)
    pre_grad = (hidden_grad * lin_act * sigmoid_pre * (1.0 + pre_act * (1.0 - sigmoid_pre))).astype(
        jnp.bfloat16
    )
    lin_grad = (hidden_grad * silu_pre).astype(jnp.bfloat16)
    backward_both_grad = jnp.concatenate([pre_grad, lin_grad], axis=1)
    item_grad = jnp.dot(backward_both_grad, gate_up.T, preferred_element_type=jnp.float32).astype(
        jnp.bfloat16
    )
    dy_rows, both_grad, item_grad = (backward_dy_rows, backward_both_grad, item_grad)
    (grad_back,) = send_back((item_grad.reshape(block_shape),))
    out_items = (
        out_back.reshape(slot_total, model_width)[position].astype(jnp.float32) * gate_flat[:, None]
    )
    mixed = jnp.sum(out_items.reshape(tok_dev, top_count, model_width), axis=1).astype(jnp.bfloat16)
    grad_items = grad_back.reshape(slot_total, model_width)[position].astype(jnp.float32)
    token_grad = jnp.sum(grad_items.reshape(tok_dev, top_count, model_width), axis=1).astype(
        jnp.bfloat16
    )
    count = lax.axis_size("dp") * weights.shape[1]
    proj_grad = jnp.dot(x_rows.T, both_grad, preferred_element_type=jnp.float32)
    down_grad = jnp.dot(dy_rows.T, hidden, preferred_element_type=jnp.float32)
    grad_sum = lax.psum_scatter(
        jnp.concatenate(
            [proj_grad.reshape(count, 2, hidden_width), down_grad.reshape(count, 1, hidden_width)],
            axis=1,
        ).astype(jnp.bfloat16),
        "dp",
        scatter_dimension=0,
        tiled=True,
    ).astype(jnp.float32)
    w_old = weights[0].astype(jnp.float32)
    m_old = first_moment[0].astype(jnp.float32)
    v_old = second_moment[0].astype(jnp.float32)
    m_new = beta_one * m_old + (1.0 - beta_one) * grad_sum
    v_new = beta_two * v_old + (1.0 - beta_two) * grad_sum * grad_sum
    m_hat = m_new / (1.0 - beta_one**step_count)
    v_hat = v_new / (1.0 - beta_two**step_count)
    w_new = w_old - learn_rate * (m_hat / (jnp.sqrt(v_hat) + eps_adam) + decay_rate * w_old)
    pieces = (
        w_new.astype(jnp.bfloat16).reshape(experts_here, -1),
        m_new.astype(jnp.bfloat16).reshape(experts_here, -1),
        v_new.astype(jnp.bfloat16).reshape(experts_here, -1),
    )
    spread = (
        lax.all_to_all(pieces[0], "expert", split_axis=0, concat_axis=0, tiled=True),
        lax.all_to_all(pieces[1], "expert", split_axis=0, concat_axis=0, tiled=True),
        lax.all_to_all(pieces[2], "expert", split_axis=0, concat_axis=0, tiled=True),
    )
    ordered = (spread[0][partner], spread[1][partner], spread[2][partner])
    homed = (
        lax.all_to_all(ordered[0], "expert", split_axis=0, concat_axis=0, tiled=True),
        lax.all_to_all(ordered[1], "expert", split_axis=0, concat_axis=0, tiled=True),
        lax.all_to_all(ordered[2], "expert", split_axis=0, concat_axis=0, tiled=True),
    )
    new_weights = homed[0].reshape(weights.shape)
    new_first = homed[1].reshape(weights.shape)
    new_second = homed[2].reshape(weights.shape)
    return (mixed, token_grad, new_weights, new_first, new_second)


def adam(w_old, m_old, v_old, grad_sum):
    m_new = beta_one * m_old + (1.0 - beta_one) * grad_sum
    v_new = beta_two * v_old + (1.0 - beta_two) * grad_sum * grad_sum
    m_hat = m_new / (1.0 - beta_one**step_count)
    v_hat = v_new / (1.0 - beta_two**step_count)
    w_new = w_old - learn_rate * (m_hat / (jnp.sqrt(v_hat) + eps_adam) + decay_rate * w_old)
    return w_new, m_new, v_new


def move_kernel(n, count, with_table, *refs):
    partner_ref, refs = refs[0], refs[1:]
    states, refs = refs[:count], refs[count:]
    if with_table:
        table_ref, refs = refs[0], refs[1:]
    homes, refs = refs[:count], refs[count:]
    if with_table:
        table_out, refs = refs[0], refs[1:]
    spread, refs = refs[:count], refs[count:]
    ordered, send_one, recv_one, send_two, recv_two = refs[:5]
    me = lax.axis_index("expert")
    share = states[0].shape[1] // n

    def rows(number):
        return pl.ds(pl.multiple_of(number * share, share), share)

    def to_peer(src, dst, send_sem, recv_sem, step):
        return pltpu.make_async_remote_copy(
            src_ref=src,
            dst_ref=dst,
            send_sem=send_sem,
            recv_sem=recv_sem,
            device_id={"expert": lax.rem(me + step, n)},
            device_id_type=pl.DeviceIdType.MESH,
        )

    def table_copy(step):
        peer = lax.rem(me + step, n)
        return to_peer(
            table_ref.at[peer], table_out.at[me], refs[5].at[step], refs[6].at[step], step
        )

    def first(i, step):
        peer = lax.rem(me + step, n)
        return to_peer(
            states[i].at[:, rows(peer), :],
            spread[i].at[me],
            send_one.at[i, step],
            recv_one.at[i, step],
            step,
        )

    def second(i, step):
        peer = lax.rem(me + step, n)
        return to_peer(
            ordered.at[i, peer],
            homes[i].at[:, rows(me), :],
            send_two.at[i, step],
            recv_two.at[i, step],
            step,
        )

    def each(fn):
        def body(step, carry):
            fn(step)
            return carry

        lax.fori_loop(1, n, body, 0)

    barrier = pltpu.get_barrier_semaphore()
    each(
        lambda step: pl.semaphore_signal(
            barrier,
            inc=1,
            device_id={"expert": lax.rem(me + step, n)},
            device_id_type=pl.DeviceIdType.MESH,
        )
    )
    pl.semaphore_wait(barrier, n - 1)
    if with_table:
        each(lambda step: table_copy(step).start())
        table_out[me] = table_ref[me]
    for i in range(count):
        each(lambda step: first(i, step).start())
    for i in range(count):
        spread[i][me] = states[i][:, rows(me), :]
        each(lambda step: first(i, step).wait_recv())

        def pick(home, carry):
            ordered[i, home] = spread[i][partner_ref[home]]
            return carry

        lax.fori_loop(0, n, pick, 0)
        each(lambda step: second(i, step).start())
        homes[i][:, rows(me), :] = ordered[i, me]
    if with_table:
        each(lambda step: table_copy(step).wait())
    for i in range(count):
        each(lambda step: first(i, step).wait_send())
        each(lambda step: second(i, step).wait())


def move_states(states, partner, table, number):
    n = lax.axis_size("expert")
    count = len(states)
    planes, own_rows, width = states[0].shape
    share = own_rows // n
    vmem = pl.BlockSpec(memory_space=pltpu.VMEM)
    extra = [] if table is None else [table]
    sems = [pltpu.SemaphoreType.DMA((count, n))] * 4
    sems += [pltpu.SemaphoreType.DMA((n,))] * (2 * len(extra))
    moved = 2 * count * planes * own_rows * width * 2
    return pl.pallas_call(
        functools.partial(move_kernel, n, count, bool(extra)),
        out_shape=[jax.ShapeDtypeStruct(a.shape, a.dtype) for a in [*states, *extra]],
        in_specs=[pl.BlockSpec(memory_space=pltpu.SMEM)] + [vmem] * (count + len(extra)),
        out_specs=[vmem] * (count + len(extra)),
        scratch_shapes=[
            *[pltpu.VMEM((n, planes, share, width), jnp.bfloat16)] * count,
            pltpu.VMEM((count, n, planes, share, width), jnp.bfloat16),
            *sems,
        ],
        compiler_params=pltpu.CompilerParams(
            collective_id=number, has_side_effects=True, vmem_limit_bytes=32 * 2**20
        ),
        cost_estimate=pl.CostEstimate(
            flops=0, bytes_accessed=30 * moved, transcendentals=0
        ),
    )(partner, *states, *extra)


def shards_dense(
    tokens, cotangent, expert_ids, gate_weights, partner, weights, first_moment, second_moment
):
    experts_here = lax.axis_size("expert")
    tok_dev, model_width = tokens.shape
    own_rows, hidden_width = weights.shape[1], weights.shape[3]
    f32, bf16 = jnp.float32, jnp.bfloat16
    hits = expert_ids[:, :, None] == jnp.arange(experts_here, dtype=jnp.int32)[None, None, :]
    gate_table = jnp.sum(jnp.where(hits, gate_weights[:, :, None], 0.0), axis=1).T
    gate_table = jnp.broadcast_to(gate_table[:, None, :], (experts_here, 8, tok_dev))
    old = [a[0].transpose(1, 0, 2) for a in (weights, first_moment, second_moment)]
    swap = [(0, 1), (1, 0)]
    half = lax.axis_index("dp")
    w_other = lax.ppermute(old[0], "dp", swap)
    low = jnp.where(half == 0, old[0], w_other)
    high = jnp.where(half == 0, w_other, old[0])
    gathered = jnp.concatenate([low, high], axis=1)
    x_rows = lax.all_gather(tokens, "expert", axis=0, tiled=True)
    cot_rows = lax.all_gather(cotangent, "expert", axis=0, tiled=True)
    w_here, m_here, gate_all = move_states(old[:2], partner, gate_table, 0)
    gate = gate_all[:, 0, :].reshape(experts_here * tok_dev, 1)
    gate_up = jnp.concatenate([gathered[0], gathered[1]], axis=1)
    down_proj = gathered[2]
    both_proj = jnp.dot(x_rows, gate_up, preferred_element_type=f32)
    pre_act = both_proj[:, :hidden_width]
    lin_act = both_proj[:, hidden_width:]
    sigmoid_pre = jax.nn.sigmoid(pre_act)
    silu_pre = pre_act * sigmoid_pre
    hidden = (silu_pre * lin_act).astype(bf16)
    out_rows = jnp.dot(hidden, down_proj.T, preferred_element_type=f32)
    out_part = (gate * out_rows).astype(bf16)
    out_part, v_old = lax.optimization_barrier((out_part, old[2]))
    mixed = lax.psum_scatter(out_part, "expert", scatter_dimension=0, tiled=True)
    (v_here,) = move_states([v_old], partner, None, 2)
    gate, v_here = lax.optimization_barrier((gate, v_here))
    dy_rows = (gate * cot_rows.astype(f32)).astype(bf16)
    hidden_grad = jnp.dot(dy_rows, down_proj, preferred_element_type=f32)
    pre_grad = hidden_grad * lin_act * sigmoid_pre * (1.0 + pre_act * (1.0 - sigmoid_pre))
    pre_grad = pre_grad.astype(bf16)
    lin_grad = (hidden_grad * silu_pre).astype(bf16)
    both_grad = jnp.concatenate([pre_grad, lin_grad], axis=1)
    proj_grad = jnp.dot(x_rows.T, both_grad, preferred_element_type=f32).astype(bf16)
    down_grad = jnp.dot(dy_rows.T, hidden, preferred_element_type=f32).astype(bf16)
    partial = jnp.stack([proj_grad[:, :hidden_width], proj_grad[:, hidden_width:], down_grad])
    partial, mixed = lax.optimization_barrier((partial, mixed))
    keep = lax.dynamic_slice_in_dim(partial, half * own_rows, own_rows, axis=1)
    give = lax.dynamic_slice_in_dim(partial, (1 - half) * own_rows, own_rows, axis=1)
    grad_sum = (keep.astype(f32) + lax.ppermute(give, "dp", swap).astype(f32)).astype(bf16)
    item_grad = jnp.dot(both_grad, gate_up.T, preferred_element_type=f32).astype(bf16)
    token_grad = lax.psum_scatter(item_grad, "expert", scatter_dimension=0, tiled=True)
    (grad_here,) = move_states([grad_sum], partner, None, 1)
    new_state = adam(*[a.astype(f32) for a in (w_here, m_here, v_here)], grad_here.astype(f32))
    outs = [a.astype(bf16).transpose(1, 0, 2)[None] for a in new_state]
    return (mixed, token_grad, *outs)


def shards(*args):
    replica_rows = lax.axis_size("expert") * args[0].shape[0]
    if lax.axis_size("dp") == 2 and replica_rows <= 4096 and args[5].shape[1] % (16 * lax.axis_size("expert")) == 0:
        return shards_dense(*args)
    return shards_by_slot(*args)


def solution(mesh):
    in_specs = (
        P(("dp", "expert"), None),
        P(("dp", "expert"), None),
        P(("dp", "expert"), None),
        P(("dp", "expert"), None),
        P(),
        P("expert", "dp", None, None),
        P("expert", "dp", None, None),
        P("expert", "dp", None, None),
    )
    out_specs = (
        P(("dp", "expert"), None),
        P(("dp", "expert"), None),
        P("expert", "dp", None, None),
        P("expert", "dp", None, None),
        P("expert", "dp", None, None),
    )
    return jax.shard_map(shards, mesh=mesh, in_specs=in_specs, out_specs=out_specs, check_vma=False)
```
